256 devices in a mesh: row: 16 (over z, core), col: 16 (over y, x).
Axes of the slice: x: 4, y: 4, z: 8, core: 2. Of those that a mesh axis runs over, the one named last changes fastest.
Arguments:
- inputs: bfloat16 [512, 16384], P('col', 'row'), may hold values from -6 to 6
- output_gradient: bfloat16 [512, 16384], P('col', 'row'), may hold values from -6 to 6
- gate_matrix: bfloat16 [16384, 26624], P('row', 'col'), may hold values from -0.046875 to 0.046875
- up_matrix: bfloat16 [16384, 26624], P('row', 'col'), may hold values from -0.046875 to 0.046875
- down_matrix: bfloat16 [26624, 16384], P('col', 'row'), may hold values from -0.046875 to 0.046875
- gate_adapter_first: bfloat16 [16384, 512], P('row', 'col'), may hold values from -0.046875 to 0.046875
- gate_adapter_second: bfloat16 [512, 26624], P('row', 'col'), may hold values from -0.25 to 0.25
- up_adapter_first: bfloat16 [16384, 512], P('row', 'col'), may hold values from -0.046875 to 0.046875
- up_adapter_second: bfloat16 [512, 26624], P('row', 'col'), may hold values from -0.25 to 0.25
- down_adapter_first: bfloat16 [26624, 512], P('col', 'row'), may hold values from -0.25 to 0.25
- down_adapter_second: bfloat16 [512, 16384], P('col', 'row'), may hold values from -0.046875 to 0.046875
Outputs:
- input_grad: bfloat16 [512, 16384], P('col', 'row')
- grad_gate_in: float32 [16384, 512], P('row', 'col')
- grad_gate_out: float32 [512, 26624], P('row', 'col')
- grad_up_in: float32 [16384, 512], P('row', 'col')
- grad_up_out: float32 [512, 26624], P('row', 'col')
- grad_down_in: float32 [26624, 512], P('col', 'row')
- grad_down_out: float32 [512, 16384], P('col', 'row')
The draws below stay inside these ranges and needn't reach their ends.
All inputs are finite; a program needn't handle non-finite values.
Results may differ from the reference program's by a relative error of at most 0.0062.
Values may be sent and summed in bfloat16 or wider, within the bound.
No kernel may reach another device: no remote copies, remote signals or barrier semaphores. Data moves between devices by JAX's collectives and lax.ppermute only.
A program may use at most 128 MiB of HBM per device.

```python
import jax
import jax.numpy as jnp
from jax import lax

MODEL_WIDTH = 16384
HIDDEN_UNITS = 26624
ADAPTER_RANK = 512
TOKENS = 512


def steps_of(stream_key, shape, shards, least, top_value):
    def one(position, shards_of):
        draws = jax.random.uniform(jax.random.fold_in(jax.random.fold_in(stream_key, 6), position), (shards_of,), jnp.float32, least / len(shards), top_value / len(shards))
        return jnp.repeat(jnp.exp(draws), shape[position] // shards_of).reshape((-1,) + (1,) * (len(shape) - position - 1))

    loudness = one(*shards[0])
    for cut in shards[1:]:
        loudness = loudness * one(*cut)
    return loudness


def centred(own_key, extent, deviation, most, split=(), held_as=jnp.bfloat16):
    values = deviation * jax.random.normal(own_key, extent, jnp.float32)
    if split:
        values = values * steps_of(own_key, extent, split, -0.22, 0.18)
    return jnp.clip(values, -most, most).astype(held_as)


def setup_inputs(seed: int = 0) -> dict:
    seeds = jax.random.split(jax.random.key(seed), 12)
    inputs = centred(seeds[0], (TOKENS, MODEL_WIDTH), 1.0, 6.0, ((0, 16), (1, 16)))
    output_gradient = centred(seeds[1], (TOKENS, MODEL_WIDTH), 1.0, 6.0, ((0, 16), (1, 16)))
    gate_matrix = centred(seeds[2], (MODEL_WIDTH, HIDDEN_UNITS), MODEL_WIDTH ** -0.5, 0.046875, ((0, 16), (1, 16)))
    up_matrix = centred(seeds[3], (MODEL_WIDTH, HIDDEN_UNITS), MODEL_WIDTH ** -0.5, 0.046875, ((0, 16), (1, 16)))
    down_matrix = centred(seeds[4], (HIDDEN_UNITS, MODEL_WIDTH), MODEL_WIDTH ** -0.5, 0.046875, ((0, 16), (1, 16)))
    gate_adapter_first = centred(seeds[5], (MODEL_WIDTH, ADAPTER_RANK), MODEL_WIDTH ** -0.5, 0.046875, ((0, 16), (1, 16)))
    gate_adapter_second = centred(seeds[6], (ADAPTER_RANK, HIDDEN_UNITS), ADAPTER_RANK ** -0.5, 0.25, ((0, 16), (1, 16)))
    up_adapter_first = centred(seeds[7], (MODEL_WIDTH, ADAPTER_RANK), MODEL_WIDTH ** -0.5, 0.046875, ((0, 16), (1, 16)))
    up_adapter_second = centred(seeds[8], (ADAPTER_RANK, HIDDEN_UNITS), ADAPTER_RANK ** -0.5, 0.25, ((0, 16), (1, 16)))
    down_adapter_first = centred(seeds[9], (HIDDEN_UNITS, ADAPTER_RANK), ADAPTER_RANK ** -0.5, 0.25, ((0, 16), (1, 16)))
    down_adapter_second = centred(seeds[10], (ADAPTER_RANK, MODEL_WIDTH), MODEL_WIDTH ** -0.5, 0.046875, ((0, 16), (1, 16)))
    return {"inputs": inputs, "output_gradient": output_gradient, "gate_matrix": gate_matrix, "up_matrix": up_matrix, "down_matrix": down_matrix, "gate_adapter_first": gate_adapter_first, "gate_adapter_second": gate_adapter_second, "up_adapter_first": up_adapter_first, "up_adapter_second": up_adapter_second, "down_adapter_first": down_adapter_first, "down_adapter_second": down_adapter_second}


def matrix_product(first_mat, second_mat):
    return jnp.dot(first_mat, second_mat, preferred_element_type=jnp.float32)


def product_transposed(first_mat, second_mat):
    return lax.dot_general(first_mat, second_mat, (((1,), (1,)), ((), ())), preferred_element_type=jnp.float32)


def product_tn(first_mat, second_mat):
    return lax.dot_general(first_mat, second_mat, (((0,), (0,)), ((), ())), preferred_element_type=jnp.float32)


def gated_back(gate_pre, up_pre, hid_grad):
    sigmoid_g = jax.nn.sigmoid(gate_pre)
    silu_g = gate_pre * sigmoid_g
    hidden_state = (silu_g * up_pre).astype(jnp.bfloat16)
    gate_gradient = (hid_grad * up_pre * sigmoid_g * (1.0 + gate_pre * (1.0 - sigmoid_g))).astype(jnp.bfloat16)
    up_gradient = (hid_grad * silu_g).astype(jnp.bfloat16)
    return hidden_state, gate_gradient, up_gradient


def reference(inputs, output_gradient, gate_matrix, up_matrix, down_matrix, gate_adapter_first, gate_adapter_second, up_adapter_first, up_adapter_second, down_adapter_first, down_adapter_second):
    reduced_gate = matrix_product(inputs, gate_adapter_first).astype(jnp.bfloat16)
    reduced_up = matrix_product(inputs, up_adapter_first).astype(jnp.bfloat16)
    reduced_cotangent = product_transposed(output_gradient, down_adapter_second).astype(jnp.bfloat16)
    gate_pre = matrix_product(inputs, gate_matrix) + matrix_product(reduced_gate, gate_adapter_second)
    up_pre = matrix_product(inputs, up_matrix) + matrix_product(reduced_up, up_adapter_second)
    hid_grad = product_transposed(output_gradient, down_matrix) + product_transposed(reduced_cotangent, down_adapter_first)
    hidden_state, gate_gradient, up_gradient = gated_back(gate_pre, up_pre, hid_grad)
    gate_reduced_gradient = product_transposed(gate_gradient, gate_adapter_second).astype(jnp.bfloat16)
    up_reduced_gradient = product_transposed(up_gradient, up_adapter_second).astype(jnp.bfloat16)
    hidden_reduced = matrix_product(hidden_state, down_adapter_first).astype(jnp.bfloat16)
    total = product_transposed(gate_gradient, gate_matrix) + product_transposed(up_gradient, up_matrix)
    total = total + product_transposed(gate_reduced_gradient, gate_adapter_first) + product_transposed(up_reduced_gradient, up_adapter_first)
    input_grad = total.astype(jnp.bfloat16)
    grad_gate_in = product_tn(inputs, gate_reduced_gradient)
    grad_gate_out = product_tn(reduced_gate, gate_gradient)
    grad_up_in = product_tn(inputs, up_reduced_gradient)
    grad_up_out = product_tn(reduced_up, up_gradient)
    grad_down_in = product_tn(hidden_state, reduced_cotangent)
    grad_down_out = product_tn(hidden_reduced, output_gradient)
    return (input_grad, grad_gate_in, grad_gate_out, grad_up_in, grad_up_out, grad_down_in, grad_down_out)
```

```python
import jax
import jax.numpy as jnp
from jax import lax
from jax.sharding import Mesh, PartitionSpec as P


F32 = jnp.float32
BF16 = jnp.bfloat16
ROW = ("z", "c")
COL = ("y", "x")


def dot_nn(a, b):
    return jnp.dot(a, b, preferred_element_type=F32)


def dot_nt(a, b):
    return lax.dot_general(a, b, (((1,), (1,)), ((), ())), preferred_element_type=F32)


def dot_tn(a, b):
    return lax.dot_general(a, b, (((0,), (0,)), ((), ())), preferred_element_type=F32)


def shift(n, d):
    return [(i, (i + d) % n) for i in range(n)]


def gather_by_exchange(block, axis, n):
    return lax.all_to_all(jnp.broadcast_to(block[None], (n,) + block.shape), axis, 0, 0)


def ring_reduce_scatter(parts, nz):
    z = lax.axis_index("z")

    def part(offset):
        return lax.dynamic_index_in_dim(parts, (z + offset) % nz, 0, keepdims=False)

    up = nz // 2
    down = nz - 1 - up
    fw = part(up).astype(BF16)
    bw = part(-down).astype(BF16)
    for k in range(up - 1, -1, -1):
        fw = lax.ppermute(fw, "z", shift(nz, 1))
        if k < down:
            bw = lax.ppermute(bw, "z", shift(nz, -1))
        if k > 0:
            fw = (fw.astype(F32) + part(k)).astype(BF16)
            if k < down:
                bw = (bw.astype(F32) + part(-k)).astype(BF16)
    return fw.astype(F32) + bw.astype(F32) + part(0)


def gated_back(gate_pre, up_pre, hid_grad):
    sig = jax.nn.sigmoid(gate_pre)
    silu = gate_pre * sig
    hidden = (silu * up_pre).astype(BF16)
    gate_grad = (hid_grad * up_pre * sig * (1.0 + gate_pre * (1.0 - sig))).astype(BF16)
    up_grad = (hid_grad * silu).astype(BF16)
    return hidden, gate_grad, up_grad


def on_device(sizes, x_blk, g_blk, wg, wu, wd, ag1, ag2, au1, au2, ad1, ad2):
    nz, nc, ny, nx = sizes
    nrow, ncol = nz * nc, ny * nx
    t, m = x_blk.shape
    rank, f = ag2.shape
    tokens = t * ncol
    tr = tokens // nrow
    ranks = rank * nrow
    core = lax.axis_index("c")

    second = lax.all_gather(
        jnp.concatenate([ag2, au2, ad1.T], axis=1), ROW, axis=0, tiled=True
    )
    first = lax.all_gather(jnp.concatenate([ag1.T, au1.T], axis=1), COL, axis=0, tiled=True)

    xg = jnp.concatenate([x_blk, g_blk], axis=1)
    xg = gather_by_exchange(xg, "x", nx).reshape(nx * t, 2 * m)
    xg = gather_by_exchange(xg, "y", ny).reshape(tokens, 2 * m)
    xs, gs = xg[:, :m], xg[:, m:]

    low_part = jnp.concatenate([dot_nn(xs, ag1), dot_nn(xs, au1), dot_nt(gs, ad2)], axis=1)
    low = lax.all_to_all(low_part.reshape(nrow, tr, 3 * rank), ROW, 0, 0).sum(0).astype(BF16)
    low = gather_by_exchange(low, COL, ncol)
    low = low.reshape(ncol, tr, 3, rank).transpose(2, 1, 0, 3)
    low_tok = low.reshape(3, tr, ranks)
    low_send = low.transpose(2, 1, 0, 3).reshape(nrow, tr, 3 * rank)
    low_slice = lax.all_to_all(low_send, ROW, 0, 0).reshape(tokens, 3 * rank)

    part = jnp.concatenate([dot_nn(xs, wg), dot_nn(xs, wu), dot_nt(gs, wd)], axis=1)
    part = part.reshape(nz, nc, tr, 3 * f)
    send = lax.dynamic_index_in_dim(part, 1 - core, 1, keepdims=False).astype(BF16)
    keep = lax.dynamic_index_in_dim(part, core, 1, keepdims=False)
    keep = keep + lax.ppermute(send, "c", shift(nc, 1)).astype(F32)
    pre = ring_reduce_scatter(keep, nz)

    gate_pre = pre[:, :f] + dot_nn(low_tok[0], second[:, :f])
    up_pre = pre[:, f : 2 * f] + dot_nn(low_tok[1], second[:, f : 2 * f])
    hid_grad = pre[:, 2 * f :] + dot_nn(low_tok[2], second[:, 2 * f :])
    acts = jnp.concatenate(gated_back(gate_pre, up_pre, hid_grad), axis=1)
    acts = lax.all_gather(acts, ROW, axis=0, tiled=True)
    hidden, gate_grad, up_grad = acts[:, :f], acts[:, f : 2 * f], acts[:, 2 * f :]

    gl = dot_nt(second[:, :f], gate_grad).astype(BF16)
    ul = dot_nt(second[:, f : 2 * f], up_grad).astype(BF16)
    hl = dot_nt(second[:, 2 * f :], hidden).astype(BF16)
    back = jnp.concatenate([v.reshape(ncol, rank, tokens) for v in (gl, ul, hl)], axis=1)
    back = lax.all_to_all(back, COL, 0, 0).astype(F32).sum(0).astype(BF16)
    gl_c, ul_c, hl_c = back[:rank], back[rank : 2 * rank], back[2 * rank :]

    total = dot_nt(gate_grad, wg) + dot_nt(up_grad, wu)
    total = total + dot_tn(gl, first[:, :m]) + dot_tn(ul, first[:, m:])
    total = total.astype(BF16).reshape(ny, nx, t, m).transpose(1, 0, 2, 3)
    total = lax.all_to_all(total, "x", 0, 0).astype(F32).sum(0).astype(BF16)
    input_grad = lax.all_to_all(total, "y", 0, 0).astype(F32).sum(0).astype(BF16)

    lg, lu, lb = low_slice[:, :rank], low_slice[:, rank : 2 * rank], low_slice[:, 2 * rank :]
    grad_gate_in = lax.dot_general(
        xs, gl_c, (((0,), (1,)), ((), ())), preferred_element_type=F32
    )
    grad_up_in = lax.dot_general(xs, ul_c, (((0,), (1,)), ((), ())), preferred_element_type=F32)
    grad_down_out = dot_nn(hl_c, gs)
    grad_gate_out = dot_tn(lg, gate_grad)
    grad_up_out = dot_tn(lu, up_grad)
    grad_down_in = dot_tn(hidden, lb)
    return (
        input_grad,
        grad_gate_in,
        grad_gate_out,
        grad_up_in,
        grad_up_out,
        grad_down_in,
        grad_down_out,
    )


def solution(mesh):
    nrow, ncol = mesh.devices.shape
    sizes = (nrow // 2, 2, 4, ncol // 4)
    fine = Mesh(mesh.devices.reshape(sizes), ("z", "c", "y", "x"))
    rc, cr = P(ROW, COL), P(COL, ROW)

    def body(*args):
        return on_device(sizes, *args)

    return jax.shard_map(
        body,
        mesh=fine,
        in_specs=(cr, cr, rc, rc, cr, rc, rc, rc, rc, cr, cr),
        out_specs=(cr, rc, rc, rc, rc, cr, cr),
        check_vma=False,
    )
```

```python
import jax
import jax.numpy as jnp
from jax import lax
from jax.sharding import Mesh, PartitionSpec as P


F32 = jnp.float32
BF16 = jnp.bfloat16
ROW = ("z", "c")
COL = ("y", "x")


def dot_nn(a, b):
    return jnp.dot(a, b, preferred_element_type=F32)


def dot_nt(a, b):
    return lax.dot_general(a, b, (((1,), (1,)), ((), ())), preferred_element_type=F32)


def dot_tn(a, b):
    return lax.dot_general(a, b, (((0,), (0,)), ((), ())), preferred_element_type=F32)


def shift(n, d):
    return [(i, (i + d) % n) for i in range(n)]


def gather_by_exchange(block, axis, n):
    return lax.all_to_all(jnp.broadcast_to(block[None], (n,) + block.shape), axis, 0, 0)


def place(blocks, axis, n):
    i = lax.axis_index(axis)
    out = jnp.zeros((n,) + blocks[0].shape, blocks[0].dtype)
    for d, b in enumerate(blocks):
        out = lax.dynamic_update_index_in_dim(out, b, (i - d) % n, 0)
    return out


def send_all(block, axis, n):
    return [block] + [lax.ppermute(block, axis, shift(n, d)) for d in range(1, n)]


def reduce_blocks(blocks, dim, axis, n):
    i = lax.axis_index(axis)

    def block(d):
        return lax.dynamic_index_in_dim(blocks, (i + d) % n, dim, keepdims=False)

    got = [lax.ppermute(block(d).astype(BF16), axis, shift(n, d)) for d in range(1, n)]
    return block(0).astype(F32) + sum(v.astype(F32) for v in got)


def ring_reduce_scatter(parts, nz):
    z = lax.axis_index("z")

    def part(offset):
        i = (z + offset) % nz
        return jnp.stack([lax.dynamic_index_in_dim(p, i, 0, keepdims=False) for p in parts])

    up = nz // 2
    down = nz - 1 - up
    fw = part(up).astype(BF16)
    bw = part(-down).astype(BF16)
    for k in range(up - 1, -1, -1):
        fw = lax.ppermute(fw, "z", shift(nz, 1))
        if k < down:
            bw = lax.ppermute(bw, "z", shift(nz, -1))
        if k > 0:
            fw = (fw.astype(F32) + part(k)).astype(BF16)
            if k < down:
                bw = (bw.astype(F32) + part(-k)).astype(BF16)
    z0 = [lax.dynamic_index_in_dim(p, z, 0, keepdims=False) for p in parts]
    return [fw[i].astype(F32) + bw[i].astype(F32) + z0[i] for i in range(len(parts))]


def gated_back(gate_pre, up_pre, hid_grad):
    sig = jax.nn.sigmoid(gate_pre)
    silu = gate_pre * sig
    hidden = (silu * up_pre).astype(BF16)
    gate_grad = (hid_grad * up_pre * sig * (1.0 + gate_pre * (1.0 - sig))).astype(BF16)
    up_grad = (hid_grad * silu).astype(BF16)
    return hidden, gate_grad, up_grad


def on_device(sizes, x_blk, g_blk, wg, wu, wd, ag1, ag2, au1, au2, ad1, ad2):
    nz, nc, ny, nx = sizes
    nrow, ncol = nz * nc, ny * nx
    t, m = x_blk.shape
    rank, f = ag2.shape
    tokens = t * ncol
    tr = tokens // nrow
    ranks = rank * nrow
    core = lax.axis_index("c")

    second = lax.all_gather(
        jnp.concatenate([ag2, au2, ad1.T], axis=1), ROW, axis=0, tiled=True
    )
    first = lax.all_gather(jnp.concatenate([ag1.T, au1.T], axis=1), COL, axis=0, tiled=True)

    xl = send_all(x_blk, "x", nx)
    gl = send_all(g_blk, "y", ny)
    xl = send_all(place(xl, "x", nx), "y", ny)
    gl = send_all(place(gl, "y", ny), "x", nx)
    xs = place(xl, "y", ny).reshape(tokens, m)
    gs = place(gl, "x", nx).transpose(1, 0, 2, 3).reshape(tokens, m)

    def half(v, i):
        v = v.reshape(nz, nc, tr, m)
        return lax.dynamic_index_in_dim(v, i, 1, keepdims=False).reshape(nz * tr, m)

    xo, go = half(xs, 1 - core), half(gs, 1 - core)
    xk, gk = half(xs, core), half(gs, core)
    keep = []
    for dot, u, v, w in ((dot_nn, xo, xk, wg), (dot_nn, xo, xk, wu), (dot_nt, go, gk, wd)):
        got = lax.ppermute(dot(u, w).astype(BF16), "c", shift(nc, 1))
        keep.append((dot(v, w) + got.astype(F32)).reshape(nz, tr, f))
    low_part = jnp.concatenate([dot_nn(xs, ag1), dot_nn(xs, au1), dot_nt(gs, ad2)], axis=1)
    keep, low_part = lax.optimization_barrier((keep, low_part))
    low = lax.all_to_all(low_part.reshape(nrow, tr, 3 * rank), ROW, 0, 0).sum(0).astype(BF16)
    low = gather_by_exchange(low.T, COL, ncol)
    lows = [low[:, i * rank : (i + 1) * rank].reshape(ranks, tr) for i in range(3)]
    gate_pre, up_pre, hid_grad = ring_reduce_scatter(keep, nz)

    gate_pre = gate_pre + dot_tn(lows[0], second[:, :f])
    up_pre = up_pre + dot_tn(lows[1], second[:, f : 2 * f])
    hid_grad = hid_grad + dot_tn(lows[2], second[:, 2 * f :])
    acts = jnp.concatenate(gated_back(gate_pre, up_pre, hid_grad), axis=1)
    acts, first, low = lax.optimization_barrier((acts, first, low))
    acts = lax.all_gather(acts, ROW, axis=0, tiled=True)
    low_slice = lax.all_to_all(low.transpose(0, 2, 1), ROW, 0, 0).reshape(tokens, 3 * rank)
    acts, low_slice = lax.optimization_barrier((acts, low_slice))
    hidden, gate_grad, up_grad = acts[:, :f], acts[:, f : 2 * f], acts[:, 2 * f :]

    gl = dot_nt(second[:, :f], gate_grad).astype(BF16)
    ul = dot_nt(second[:, f : 2 * f], up_grad).astype(BF16)
    hl = dot_nt(second[:, 2 * f :], hidden).astype(BF16)
    back = jnp.concatenate([v.reshape(ncol, rank, tokens) for v in (gl, ul, hl)], axis=1)
    back, gate_later, up_later = lax.optimization_barrier((back, gate_grad, up_grad))
    back = reduce_blocks(back.reshape(ny, nx, 3 * rank, tokens), 0, "y", ny)
    back = reduce_blocks(back, 0, "x", nx).astype(BF16)
    gl_c, ul_c, hl_c = back[:rank], back[rank : 2 * rank], back[2 * rank :]

    total = dot_nt(gate_later, wg) + dot_nt(up_later, wu)
    total = total + dot_tn(gl, first[:, :m]) + dot_tn(ul, first[:, m:])
    total = reduce_blocks(total.reshape(ny, nx, t, m), 1, "x", nx)
    input_grad = reduce_blocks(total, 0, "y", ny).astype(BF16)

    lg, lu, lb = low_slice[:, :rank], low_slice[:, rank : 2 * rank], low_slice[:, 2 * rank :]
    grad_gate_in = lax.dot_general(
        xs, gl_c, (((0,), (1,)), ((), ())), preferred_element_type=F32
    )
    grad_up_in = lax.dot_general(xs, ul_c, (((0,), (1,)), ((), ())), preferred_element_type=F32)
    grad_down_out = dot_nn(hl_c, gs)
    grad_gate_out = dot_tn(lg, gate_grad)
    grad_up_out = dot_tn(lu, up_grad)
    grad_down_in = dot_tn(hidden, lb)
    return (
        input_grad,
        grad_gate_in,
        grad_gate_out,
        grad_up_in,
        grad_up_out,
        grad_down_in,
        grad_down_out,
    )


def solution(mesh):
    nrow, ncol = mesh.devices.shape
    sizes = (nrow // 2, 2, 4, ncol // 4)
    fine = Mesh(mesh.devices.reshape(sizes), ("z", "c", "y", "x"))
    rc, cr = P(ROW, COL), P(COL, ROW)

    def body(*args):
        return on_device(sizes, *args)

    return jax.shard_map(
        body,
        mesh=fine,
        in_specs=(cr, cr, rc, rc, cr, rc, rc, rc, rc, cr, cr),
        out_specs=(cr, rc, rc, rc, rc, cr, cr),
        check_vma=False,
    )
```

```python
import jax
import jax.numpy as jnp
from jax import lax
from jax.experimental import pallas as pl
from jax.experimental.pallas import tpu as pltpu
from jax.sharding import Mesh, PartitionSpec as P


F32 = jnp.float32
BF16 = jnp.bfloat16
ROW = ("z", "c")
COL = ("y", "x")
SCALARS = pl.BlockSpec(memory_space=pltpu.SMEM)
VECTORS = pl.BlockSpec(memory_space=pltpu.VMEM)


def dot_nn(a, b):
    return jnp.dot(a, b, preferred_element_type=F32)


def dot_nt(a, b):
    return lax.dot_general(a, b, (((1,), (1,)), ((), ())), preferred_element_type=F32)


def dot_tn(a, b):
    return lax.dot_general(a, b, (((0,), (0,)), ((), ())), preferred_element_type=F32)


def shift(n, d):
    return [(i, (i + d) % n) for i in range(n)]


def gather_by_exchange(block, axis, n):
    return lax.all_to_all(jnp.broadcast_to(block[None], (n,) + block.shape), axis, 0, 0)


def in_order(xl, gl, nz, ny, nx):
    ncol, (t, m) = ny * nx, xl[0].shape[1:]
    pos = jnp.stack([lax.axis_index(v) for v in ("z", "c", "y", "x")]).astype(jnp.int32)

    def kernel(pos_ref, *refs):
        x_in, g_in = refs[:ny], refs[ny : ny + nx]
        outs = refs[ny + nx :]
        z, c, y, x = (pos_ref[i] for i in range(4))
        for d in range(ny):
            for e in range(nx):
                outs[0][((y + (ny - d)) % ny) * nx + (x + (nx - e)) % nx] = x_in[d][e]
        for d in range(nx):
            for e in range(ny):
                outs[1][((y + (ny - e)) % ny) * nx + (x + (nx - d)) % nx] = g_in[d][e]
        for j in range(nz):
            mine = ((z + j) % nz) * 2
            for i in range(2):
                outs[2 + i][j] = outs[i][mine + c]
                outs[4 + i][j] = outs[i][mine + (1 - c)]

    return pl.pallas_call(
        kernel,
        out_shape=[jax.ShapeDtypeStruct((ncol, t, m), BF16)] * 2
        + [jax.ShapeDtypeStruct((nz, t, m), BF16)] * 4,
        in_specs=[SCALARS] + [VECTORS] * (ny + nx),
        out_specs=[VECTORS] * 6,
        name="in_order",
    )(pos, *xl, *gl)


def activations(parts, fw, bw, low, second):
    n, (_, t, w) = len(parts), parts[0].shape
    ncol, rank = low.shape[0], low.shape[1] // n

    def kernel(p0, p1, p2, fw_ref, bw_ref, low_ref, sec_ref, out):
        pre = []
        for j, p in enumerate((p0, p1, p2)):
            lo = low_ref[:, j * rank : (j + 1) * rank, :].reshape(ncol * rank, t)
            v = p[0] + fw_ref[j].astype(F32) + bw_ref[j].astype(F32)
            pre.append(v + dot_tn(lo, sec_ref[:, j * w : (j + 1) * w]))
        for j, v in enumerate(gated_back(*pre)):
            out[:, j * w : (j + 1) * w] = v

    return pl.pallas_call(
        kernel,
        out_shape=jax.ShapeDtypeStruct((t, n * w), BF16),
        grid=(1,),
        in_specs=[pl.BlockSpec((1, t, w), lambda g: (0, 0, 0))] * n
        + [pl.BlockSpec(v.shape, lambda g, nd=v.ndim: (0,) * nd) for v in (fw, bw, low, second)],
        out_specs=pl.BlockSpec((t, n * w), lambda g: (0, 0)),
        name="activations",
    )(*parts, fw, bw, low, second)


def send_all(block, axis, n):
    return [block] + [lax.ppermute(block, axis, shift(n, d)) for d in range(1, n)]


def reduce_blocks(blocks, dim, axis, n):
    i = lax.axis_index(axis)

    def block(d):
        return lax.dynamic_index_in_dim(blocks, (i + d) % n, dim, keepdims=False)

    got = [lax.ppermute(block(d).astype(BF16), axis, shift(n, d)) for d in range(1, n)]
    return block(0).astype(F32) + sum(v.astype(F32) for v in got)


def after(value, *others):
    return lax.optimization_barrier((value,) + others)[0]


def gated_back(gate_pre, up_pre, hid_grad):
    sig = jax.nn.sigmoid(gate_pre)
    silu = gate_pre * sig
    hidden = (silu * up_pre).astype(BF16)
    gate_grad = (hid_grad * up_pre * sig * (1.0 + gate_pre * (1.0 - sig))).astype(BF16)
    up_grad = (hid_grad * silu).astype(BF16)
    return hidden, gate_grad, up_grad


def on_device(sizes, x_blk, g_blk, wg, wu, wd, ag1, ag2, au1, au2, ad1, ad2):
    nz, nc, ny, nx = sizes
    nrow, ncol = nz * nc, ny * nx
    t, m = x_blk.shape
    rank, f = ag2.shape
    tokens = t * ncol
    tr = tokens // nrow

    second = jnp.concatenate([ag2, au2, ad1.T], axis=1)
    first = jnp.concatenate([ag1.T, au1.T], axis=1)
    second = lax.all_gather(second, ROW, axis=0, tiled=True)
    first = lax.all_gather(first, COL, axis=0, tiled=True)

    xl = send_all(x_blk, "x", nx)
    gl = send_all(g_blk, "y", ny)
    xl = send_all(jnp.stack(xl), "y", ny)
    gl = send_all(jnp.stack(gl), "x", nx)
    blocks = in_order(xl, gl, nz, ny, nx)
    xs, gs, xk, gk, xo, go = (v.reshape(-1, m) for v in blocks)

    keep = []
    for dot, u, v, w in ((dot_nn, xo, xk, wg), (dot_nn, xo, xk, wu), (dot_nt, go, gk, wd)):
        got = lax.ppermute(dot(u, w).astype(BF16), "c", shift(nc, 1))
        keep.append((dot(v, w) + got.astype(F32)).reshape(nz, tr, f))
    low_part = jnp.concatenate(
        [dot_nn(xs, ag1), dot_nn(xs, au1), dot_nt(gs, ad2)], axis=1
    )

    def message(offset, got=None):
        v = jnp.stack([p[offset % nz] for p in keep])
        return (v if got is None else v + got.astype(F32)).astype(BF16)

    up, down = nz // 2, nz - 1 - nz // 2
    low = low_part.reshape(nrow, tr, 3 * rank)
    fw, bw = message(up), message(-down)
    for k in range(up - 1, -1, -1):
        if k == up - 1:
            low = lax.all_to_all(after(low, fw, bw), ROW, 0, 0)
        if k == up - 2:
            low = after(low, fw, bw).sum(0).astype(BF16).T
            low = gather_by_exchange(low, COL, ncol)
        fw = lax.ppermute(fw, "z", shift(nz, 1))
        if up - k <= down:
            bw = lax.ppermute(bw, "z", shift(nz, -1))
        if k > 0:
            fw = message(k, fw)
            if up - k < down:
                bw = message(up - k - down, bw)
    acts = activations(keep, fw, bw, low, second)
    acts, first = lax.optimization_barrier((acts, first))
    low = after(low, acts)
    acts = lax.all_gather(acts, ROW, axis=0, tiled=True)
    low_slice = lax.all_to_all(low.transpose(0, 2, 1), ROW, 0, 0).reshape(tokens, 3 * rank)
    sec = after(second, low)
    sec = [sec[:, i * f : (i + 1) * f] for i in range(3)]
    acts, low_slice, sg, su, sd = lax.optimization_barrier((acts, low_slice, *sec))
    hidden, gate_grad, up_grad = acts[:, :f], acts[:, f : 2 * f], acts[:, 2 * f :]

    gl = dot_nt(sg, gate_grad).astype(BF16)
    ul = dot_nt(su, up_grad).astype(BF16)
    hl = dot_nt(sd, hidden).astype(BF16)
    back = jnp.concatenate([v.reshape(ncol, rank, tokens) for v in (gl, ul, hl)], axis=1)
    back, gate_later, up_later = lax.optimization_barrier((back, gate_grad, up_grad))
    back = reduce_blocks(back.reshape(ny, nx, 3 * rank, tokens), 0, "y", ny)
    back = reduce_blocks(back, 0, "x", nx).astype(BF16)
    gl_c, ul_c, hl_c = back[:rank], back[rank : 2 * rank], back[2 * rank :]

    total = dot_nt(gate_later, wg) + dot_nt(up_later, wu)
    total = total + dot_tn(gl, first[:, :m]) + dot_tn(ul, first[:, m:])
    low_slice = after(low_slice, total)
    total = reduce_blocks(total.reshape(ny, nx, t, m), 1, "x", nx)
    input_grad = reduce_blocks(total, 0, "y", ny).astype(BF16)

    lg, lu, lb = low_slice[:, :rank], low_slice[:, rank : 2 * rank], low_slice[:, 2 * rank :]
    grad_gate_in = lax.dot_general(
        xs, gl_c, (((0,), (1,)), ((), ())), preferred_element_type=F32
    )
    grad_up_in = lax.dot_general(xs, ul_c, (((0,), (1,)), ((), ())), preferred_element_type=F32)
    grad_down_out = dot_nn(hl_c, gs)
    grad_gate_out = dot_tn(lg, gate_grad)
    grad_up_out = dot_tn(lu, up_grad)
    grad_down_in = dot_tn(hidden, lb)
    return (
        input_grad,
        grad_gate_in,
        grad_gate_out,
        grad_up_in,
        grad_up_out,
        grad_down_in,
        grad_down_out,
    )


def solution(mesh):
    nrow, ncol = mesh.devices.shape
    sizes = (nrow // 2, 2, 4, ncol // 4)
    fine = Mesh(mesh.devices.reshape(sizes), ("z", "c", "y", "x"))
    rc, cr = P(ROW, COL), P(COL, ROW)

    def body(*args):
        return on_device(sizes, *args)

    return jax.shard_map(
        body,
        mesh=fine,
        in_specs=(cr, cr, rc, rc, cr, rc, rc, rc, rc, cr, cr),
        out_specs=(cr, rc, rc, rc, rc, cr, cr),
        check_vma=False,
    )
```

```python
import jax
import jax.numpy as jnp
from jax import lax
from jax.experimental import pallas as pl
from jax.experimental.pallas import tpu as pltpu
from jax.sharding import Mesh, PartitionSpec as P


F32 = jnp.float32
BF16 = jnp.bfloat16
ROW = ("z", "c")
COL = ("y", "x")
SCALARS = pl.BlockSpec(memory_space=pltpu.SMEM)
VECTORS = pl.BlockSpec(memory_space=pltpu.VMEM)


def dot_nn(a, b):
    return jnp.dot(a, b, preferred_element_type=F32)


def dot_nt(a, b):
    return lax.dot_general(a, b, (((1,), (1,)), ((), ())), preferred_element_type=F32)


def dot_tn(a, b):
    return lax.dot_general(a, b, (((0,), (0,)), ((), ())), preferred_element_type=F32)


def shift(n, d):
    return [(i, (i + d) % n) for i in range(n)]


def gather_by_exchange(block, axis, n):
    return lax.all_to_all(jnp.broadcast_to(block[None], (n,) + block.shape), axis, 0, 0)


def in_order(xl, gl, nz, ny, nx):
    ncol, (t, m) = ny * nx, xl[0].shape[1:]
    pos = jnp.stack([lax.axis_index(v) for v in ("z", "c", "y", "x")]).astype(jnp.int32)

    def kernel(pos_ref, *refs):
        x_in, g_in = refs[:ny], refs[ny : ny + nx]
        outs = refs[ny + nx :]
        z, c, y, x = (pos_ref[i] for i in range(4))
        for d in range(ny):
            for e in range(nx):
                outs[0][((y + (ny - d)) % ny) * nx + (x + (nx - e)) % nx] = x_in[d][e]
        for d in range(nx):
            for e in range(ny):
                outs[1][((y + (ny - e)) % ny) * nx + (x + (nx - d)) % nx] = g_in[d][e]
        for j in range(nz):
            mine = ((z + j) % nz) * 2
            for i in range(2):
                outs[2 + i][j] = outs[i][mine + c]
                outs[4 + i][j] = outs[i][mine + (1 - c)]

    return pl.pallas_call(
        kernel,
        out_shape=[jax.ShapeDtypeStruct((ncol, t, m), BF16)] * 2
        + [jax.ShapeDtypeStruct((nz, t, m), BF16)] * 4,
        in_specs=[SCALARS] + [VECTORS] * (ny + nx),
        out_specs=[VECTORS] * 6,
        name="in_order",
    )(pos, *xl, *gl)


def activations(parts, fw, bw, low, second):
    n, (_, t, w) = len(parts), parts[0].shape
    ncol, rank = low.shape[0], low.shape[1] // n

    def kernel(p0, p1, p2, fw_ref, bw_ref, low_ref, sec_ref, out):
        pre = []
        for j, p in enumerate((p0, p1, p2)):
            lo = low_ref[:, j * rank : (j + 1) * rank, :].reshape(ncol * rank, t)
            v = p[0] + fw_ref[j].astype(F32) + bw_ref[j].astype(F32)
            pre.append(v + dot_tn(lo, sec_ref[:, j * w : (j + 1) * w]))
        for j, v in enumerate(gated_back(*pre)):
            out[:, j * w : (j + 1) * w] = v

    return pl.pallas_call(
        kernel,
        out_shape=jax.ShapeDtypeStruct((t, n * w), BF16),
        grid=(1,),
        in_specs=[pl.BlockSpec((1, t, w), lambda g: (0, 0, 0))] * n
        + [pl.BlockSpec(v.shape, lambda g, nd=v.ndim: (0,) * nd) for v in (fw, bw, low, second)],
        out_specs=pl.BlockSpec((t, n * w), lambda g: (0, 0)),
        name="activations",
    )(*parts, fw, bw, low, second)


def send_all(block, axis, n):
    return [block] + [lax.ppermute(block, axis, shift(n, d)) for d in range(1, n)]


def reduce_blocks(blocks, dim, axis, n):
    i = lax.axis_index(axis)

    def block(d):
        return lax.dynamic_index_in_dim(blocks, (i + d) % n, dim, keepdims=False)

    out = [block(d).astype(BF16) for d in range(1, n)]
    got = [lax.ppermute(v, axis, shift(n, d + 1)) for d, v in enumerate(out)]
    return block(0).astype(F32) + sum(v.astype(F32) for v in got)


def after(value, *others):
    return lax.optimization_barrier((value,) + others)[0]


def gated_back(gate_pre, up_pre, hid_grad):
    sig = jax.nn.sigmoid(gate_pre)
    silu = gate_pre * sig
    hidden = (silu * up_pre).astype(BF16)
    gate_grad = (hid_grad * up_pre * sig * (1.0 + gate_pre * (1.0 - sig))).astype(BF16)
    up_grad = (hid_grad * silu).astype(BF16)
    return hidden, gate_grad, up_grad


def on_device(sizes, x_blk, g_blk, wg, wu, wd, ag1, ag2, au1, au2, ad1, ad2):
    nz, nc, ny, nx = sizes
    nrow, ncol = nz * nc, ny * nx
    t, m = x_blk.shape
    rank, f = ag2.shape
    tokens = t * ncol
    tr = tokens // nrow

    second = jnp.concatenate([ag2, au2, ad1.T], axis=1)
    first = jnp.concatenate([ag1.T, au1.T], axis=1)
    second = lax.all_gather(second, ROW, axis=0, tiled=True)
    first = lax.all_gather(first, COL, axis=0, tiled=True)

    xl = send_all(x_blk, "x", nx)
    gl = send_all(g_blk, "y", ny)
    xl = send_all(jnp.stack(xl), "y", ny)
    gl = send_all(jnp.stack(gl), "x", nx)
    blocks = in_order(xl, gl, nz, ny, nx)
    xs, gs, xk, gk, xo, go = (v.reshape(-1, m) for v in blocks)

    keep = []
    for dot, u, v, w in ((dot_nn, xo, xk, wg), (dot_nn, xo, xk, wu), (dot_nt, go, gk, wd)):
        got = lax.ppermute(dot(u, w).astype(BF16), "c", shift(nc, 1))
        keep.append((dot(v, w) + got.astype(F32)).reshape(nz, tr, f))
    low_part = jnp.concatenate(
        [dot_nn(xs, ag1), dot_nn(xs, au1), dot_nt(gs, ad2)], axis=1
    )

    def message(offset, got=None):
        v = jnp.stack([p[offset % nz] for p in keep])
        return (v if got is None else v + got.astype(F32)).astype(BF16)

    up, down = nz // 2, nz - 1 - nz // 2
    low = low_part.reshape(nrow, tr, 3 * rank)
    fw, bw = message(up), message(-down)
    for k in range(up - 1, -1, -1):
        if k == up - 2:
            low = lax.all_to_all(after(low, fw, bw), ROW, 0, 0)
        if k == up - 3:
            low = after(low, fw, bw).sum(0).astype(BF16).T
            low = gather_by_exchange(low, COL, ncol)
        fw = lax.ppermute(fw, "z", shift(nz, 1))
        if up - k <= down:
            bw = lax.ppermute(bw, "z", shift(nz, -1))
        if k > 0:
            fw = message(k, fw)
            if up - k < down:
                bw = message(up - k - down, bw)
    acts = activations(keep, fw, bw, low, second)
    acts, first = lax.optimization_barrier((acts, first))
    low = after(low, acts)
    acts = lax.all_gather(acts, ROW, axis=0, tiled=True)
    low_slice = lax.all_to_all(low.transpose(0, 2, 1), ROW, 0, 0).reshape(tokens, 3 * rank)
    sec = after(second, low)
    sec = [sec[:, i * f : (i + 1) * f] for i in range(3)]
    acts, low_slice, sg, su, sd = lax.optimization_barrier((acts, low_slice, *sec))
    hidden, gate_grad, up_grad = acts[:, :f], acts[:, f : 2 * f], acts[:, 2 * f :]

    gl = dot_nt(sg, gate_grad).astype(BF16)
    ul = dot_nt(su, up_grad).astype(BF16)
    hl = dot_nt(sd, hidden).astype(BF16)
    back = jnp.concatenate([v.reshape(ncol, rank, tokens) for v in (gl, ul, hl)], axis=1)
    back, gate_later, up_later = lax.optimization_barrier((back, gate_grad, up_grad))
    back = reduce_blocks(back.reshape(ny, nx, 3 * rank, tokens), 0, "y", ny)
    back = reduce_blocks(back, 0, "x", nx).astype(BF16)
    gl_c, ul_c, hl_c = back[:rank], back[rank : 2 * rank], back[2 * rank :]

    total = dot_nt(gate_later, wg) + dot_nt(up_later, wu)
    total = total + dot_tn(gl, first[:, :m]) + dot_tn(ul, first[:, m:])
    low_slice = after(low_slice, total)
    total = reduce_blocks(total.reshape(ny, nx, t, m), 1, "x", nx)
    input_grad = reduce_blocks(total, 0, "y", ny).astype(BF16)

    lg, lu, lb = low_slice[:, :rank], low_slice[:, rank : 2 * rank], low_slice[:, 2 * rank :]
    grad_gate_in = lax.dot_general(xs, gl_c, (((0,), (1,)), ((), ())), preferred_element_type=F32)
    grad_up_in = lax.dot_general(xs, ul_c, (((0,), (1,)), ((), ())), preferred_element_type=F32)
    grad_down_out = dot_nn(hl_c, gs)
    grad_gate_out = dot_tn(lg, gate_grad)
    grad_up_out = dot_tn(lu, up_grad)
    grad_down_in = dot_tn(hidden, lb)
    return (
        input_grad,
        grad_gate_in,
        grad_gate_out,
        grad_up_in,
        grad_up_out,
        grad_down_in,
        grad_down_out,
    )


def solution(mesh):
    nrow, ncol = mesh.devices.shape
    sizes = (nrow // 2, 2, 4, ncol // 4)
    fine = Mesh(mesh.devices.reshape(sizes), ("z", "c", "y", "x"))
    rc, cr = P(ROW, COL), P(COL, ROW)

    def body(*args):
        return on_device(sizes, *args)

    return jax.shard_map(
        body,
        mesh=fine,
        in_specs=(cr, cr, rc, rc, cr, rc, rc, rc, rc, cr, cr),
        out_specs=(cr, rc, rc, rc, rc, cr, cr),
        check_vma=False,
    )
```
